256 devices in a mesh: col: 64 (over z, x, core), row: 4 (over y).
Axes of the slice: x: 4, y: 4, z: 8, core: 2. Of those that a mesh axis runs over, the one named last changes fastest.
Arguments:
- matrix: float32 [16, 512, 1, 8192], P(None, 'row', None, 'col'), may hold values from -1 to 5, as said below
- inverse_factors: float32 [2, 512, 512], replicated, may hold values from -1 to 1, as said below
Outputs:
- factored: float32 [16, 512, 1, 8192], P(None, 'row', None, 'col')
The draws below stay inside these ranges and needn't reach their ends.
Inputs may be any that keep to these rules, and one draw needn't show every extreme that they name: matrix holds a symmetric matrix. Each inverse_factors[k] is lower triangular with a positive diagonal; it is given independently of matrix.
All inputs are finite; a program needn't handle non-finite values.
Results may differ from the reference program's by a relative error of at most 0.0001.
Values sent between devices are 32-bit elements; how exact they have to be, the bound alone decides.
No kernel may reach another device: no remote copies, remote signals or barrier semaphores. Data moves between devices by JAX's collectives and lax.ppermute only.
A program may use at most 64 MiB of HBM per device.

```python
import jax
import jax.numpy as jnp
from jax import lax

NB = 128
P_SIZE = 512
CYC = 1
M = 8192
N_ROW = 4


def draw_matrix(key, part):
    first_key, second_key = jax.random.split(jax.random.fold_in(key, 17))
    noise = jax.random.normal(first_key, (M, M), jnp.float32)
    square = 0.05 * (noise + noise.T)
    diagonal = 2.0 + 2.0 * jax.random.uniform(second_key, (M,), jnp.float32)
    positions = jnp.arange(M)
    square = square.at[positions, positions].add(diagonal)
    return square.reshape(M // (N_ROW * NB), N_ROW * NB, CYC, M // CYC)


def draw_inverse_factors(key, part):
    first_key, second_key = jax.random.split(jax.random.fold_in(key, 29))
    indices = jnp.arange(P_SIZE)
    diag_values = 1.0 / jnp.sqrt(2.0 + 2.0 * jax.random.uniform(second_key, (2, P_SIZE), jnp.float32))
    noise = jax.random.normal(first_key, (2, P_SIZE, P_SIZE), jnp.float32)
    strict = indices[:, None] > indices[None, :]
    equal = indices[:, None] == indices[None, :]
    below = jnp.where(strict[None], 0.2 * noise / P_SIZE ** 0.5, 0.0)
    return below + jnp.where(equal[None], diag_values[:, :, None], 0.0)


def setup_inputs(seed: int = 0) -> dict:
    arg_keys = jax.random.split(jax.random.key(seed), 3)
    return {
        "matrix": draw_matrix(jax.random.fold_in(arg_keys[2], 71), 0),
        "inverse_factors": draw_inverse_factors(jax.random.fold_in(arg_keys[2], 71), 0),
    }


def exact_dot(left_side, right_side):
    return jnp.dot(left_side, right_side, precision=lax.Precision.HIGHEST, preferred_element_type=jnp.float32)


def reference(matrix, inverse_factors):
    square = matrix.reshape(M, M)
    indices = jnp.arange(M)[:, None]
    for panel in range(2):
        offset = panel * P_SIZE
        factor_cols = exact_dot(square[:, offset:offset + P_SIZE], inverse_factors[panel].T)
        trailing = jnp.where(indices >= offset + P_SIZE, factor_cols, 0.0)
        square = square - exact_dot(trailing, trailing.T)
        square = square.at[:, offset:offset + P_SIZE].set(jnp.where(indices >= offset, factor_cols, 0.0))
    return square.reshape(matrix.shape)
```

```python
import jax
import jax.numpy as jnp
from jax import lax
from jax.experimental import pallas as pl
from jax.experimental.pallas import tpu as pltpu
from jax.sharding import Mesh
from jax.sharding import PartitionSpec as P

Z, X, K, Y = 8, 4, 2, 4
B = 128
FIRST = (0, 2, 1, 3)
SECOND = (1, 3, 0, 2)


def dot(a, b, dims=((1,), (0,))):
    return lax.dot_general(
        a, b, (dims, ((), ())), precision=lax.Precision.HIGHEST, preferred_element_type=jnp.float32
    )


def shift(v, axis, size, step):
    return lax.ppermute(v, axis, [(i, (i + step) % size) for i in range(size)])


def other_core(v):
    return lax.ppermute(v, "k", [(0, 1), (1, 0)])


def swap(v, choice):
    perm = []
    for x in range(X):
        for k in range(K):
            for y in range(Y):
                source = ((2 * k + (y >> 1)) * K + (y & 1)) * Y + choice[x]
                perm.append((source, (x * K + k) * Y + y))
    return lax.ppermute(v, ("x", "k", "y"), perm)


def after(value, *done):
    return lax.optimization_barrier((value, *done))[0]


def gather_y(v, y):
    parts = [v] + [shift(v, "y", Y, s) for s in range(1, Y)]
    out = jnp.zeros((Y,) + v.shape, v.dtype)
    for s, part in enumerate(parts):
        out = lax.dynamic_update_index_in_dim(out, part, (y + Y - s) % Y, 0)
    return out


def split(v):
    high = v.astype(jnp.bfloat16)
    return high, (v - high.astype(jnp.float32)).astype(jnp.bfloat16)


def product(pos, pieces, z_main, z_alt):
    names = [(t, c) for t in range(Z) for c in range(8)]
    arrays, index = [], {}
    for name in names:
        array, at = pieces[name]
        for i, known in enumerate(arrays):
            if known is array:
                break
        else:
            i = len(arrays)
            arrays.append(array)
        index[name] = (i, at)

    def body(pos_ref, *refs):
        xs = refs[: len(arrays)]
        zm, za, own, oth, xh, xl = refs[len(arrays) :]
        for t, c in names:
            i, at = index[(t, c)]
            high, low = split(xs[i][at])
            xh[t * B : (t + 1) * B, c * B : (c + 1) * B] = high
            xl[t * B : (t + 1) * B, c * B : (c + 1) * B] = low

        def mul(h, l, z):
            zh, zl = split(z)
            f = lambda a, b: jnp.dot(a, b, preferred_element_type=jnp.float32)
            return f(h, zh) + (f(h, zl) + f(l, zh))

        mine = pos_ref[0]
        res = mul(xh[...], xl[...], zm[...])
        for t in range(Z):
            row = pl.multiple_of(lax.rem(mine + t, Z) * B, B)
            own[pl.ds(row, B), :] = res[t * B : (t + 1) * B, :B]
            oth[pl.ds(row, B), :] = res[t * B : (t + 1) * B, B:]
        at = pl.multiple_of(lax.rem(Z - mine, Z) * B, B)
        alt = mul(xh[pl.ds(at, B), :], xl[pl.ds(at, B), :], za[...])
        own[:B, :] = alt[:, :B]
        oth[:B, :] = alt[:, B:]

    vmem = pl.BlockSpec(memory_space=pltpu.VMEM)
    half = jax.ShapeDtypeStruct((Z * B, B), jnp.float32)
    return pl.pallas_call(
        body,
        out_shape=(half, half),
        in_specs=[pl.BlockSpec(memory_space=pltpu.SMEM)] + [vmem] * (len(arrays) + 2),
        out_specs=(vmem, vmem),
        scratch_shapes=[pltpu.VMEM((Z * B, 8 * B), jnp.bfloat16)] * 2,
        compiler_params=pltpu.CompilerParams(vmem_limit_bytes=40 * 2**20),
        cost_estimate=pl.CostEstimate(flops=2 * 3 * 1024 * 1024 * 256, bytes_accessed=7 * 2**20, transcendentals=0),
    )(pos, *arrays, z_main, z_alt)


def shards(matrix, inverse_factors):
    z, x, k, y = (lax.axis_index(n) for n in ("z", "x", "k", "y"))
    a = matrix.reshape(16, B, B)
    l0, l1 = inverse_factors[0], inverse_factors[1]

    blocks = jnp.swapaxes(a[:2], 1, 2)
    f0, g0 = swap(blocks, FIRST), swap(blocks, SECOND)

    def ring(v):
        up, down = [v], [v]
        for _ in range(3):
            up.append(shift(up[-1], "z", Z, 1))
            down.append(shift(down[-1], "z", Z, -1))
        return up, down

    def last(up, down):
        return shift(up[3][:1], "z", Z, 1), shift(down[3][1:], "z", Z, -1)

    def along_x(*parts):
        v = jnp.concatenate(parts)
        return shift(v, "x", X, 1), shift(v, "x", X, -1)

    fu, fd = ring(f0)
    gu, gd = ring(g0)
    fa, fb = last(fu, fd)
    ga, gb = last(gu, gd)
    x0 = along_x(f0, fu[1], fd[1])
    x1 = along_x(fu[2], fd[2])
    x2 = along_x(fu[3], fd[3], fa, fb)

    pieces = {}
    order = {0: fu[0], 1: fd[1], 2: fd[2], 3: fd[3], 5: fu[3], 6: fu[2], 7: fu[1]}
    orderg = {0: gu[0], 1: gd[1], 2: gd[2], 3: gd[3], 5: gu[3], 6: gu[2], 7: gu[1]}
    where_x = {0: (0, 0), 7: (0, 2), 1: (0, 4), 6: (1, 0), 2: (1, 2), 5: (2, 0), 3: (2, 2), 4: (2, 4)}
    xs = (x0, x1, x2)
    for t in range(Z):
        for p in range(2):
            if t == 4:
                pieces[(t, 4 * p)] = ((fa, fb)[p], 0)
                pieces[(t, 4 * p + 1)] = ((ga, gb)[p], 0)
            else:
                pieces[(t, 4 * p)] = (order[t], p)
                pieces[(t, 4 * p + 1)] = (orderg[t], p)
            n, at = where_x[t]
            pieces[(t, 4 * p + 2)] = (xs[n][0], at + p)
            pieces[(t, 4 * p + 3)] = (xs[n][1], at + p)

    mine = gather_y(a[:2], y)
    theirs = other_core(mine)
    cols = jnp.concatenate([mine, theirs], axis=3)
    ac0, ac1 = cols[:, 0].reshape(4 * B, 2 * B), cols[:, 1].reshape(4 * B, 2 * B)

    g = jnp.where(x < 2, a[1].T, a[0])
    for reach in (4, 2, 1):
        got = lax.ppermute(g, "z", [(i, i + reach) for i in range(0, Z, 2 * reach)])
        g = jnp.where(z % (2 * reach) == reach, got, g)
    got = other_core(g)
    g = jnp.stack([jnp.where(k == 0, g, got), jnp.where(k == 0, got, g)])
    got = lax.ppermute(g, "x", [(0, 1), (1, 0), (2, 3), (3, 2)])
    g = jnp.stack([jnp.where(x % 2 == 0, g, got), jnp.where(x % 2 == 0, got, g)]).reshape(4, B, B)
    g = gather_y(g, y)
    g = jnp.where(x < 2, jnp.swapaxes(g, 0, 1), g)
    gs = jnp.swapaxes(g, 1, 2).reshape(4 * B, 4 * B)

    row = lax.broadcasted_iota(jnp.int32, (4 * B, 2 * B), 0)
    col = lax.broadcasted_iota(jnp.int32, (4 * B, 2 * B), 1)
    block = 2 * (x % 2) + jnp.where(col < B, k, 1 - k)
    unit = jnp.where(row == block * B + col % B, 1.0, 0.0)
    w0 = dot(l0, ac0)
    v0 = dot(l0, w0, ((0,), (0,)))
    u1 = dot(l1, ac1 - dot(gs, v0, ((0,), (0,))))
    w0 = jnp.where(z == 0, jnp.where(x < 2, unit, 0.0), w0)
    u1 = jnp.where(z == 0, jnp.where(x < 2, 0.0, unit), u1)
    zb = dot(l1, u1, ((0,), (0,)))
    zt = dot(l0, w0 - dot(l0, dot(gs, zb)), ((0,), (0,)))
    sign = jnp.where(z == 0, -1.0, 1.0)
    full = jnp.stack([zt, zb]) * sign
    alt = jnp.where(
        z == 0,
        jnp.where((k == 1) | (x < 2), full, 0.0),
        jnp.where(k == 1, jnp.stack([v0, jnp.zeros_like(v0)]), 0.0),
    )
    first = jnp.array(FIRST)
    which = jnp.stack([first[x], jnp.array(SECOND)[x], first[(x + 3) % 4], first[(x + 1) % 4]])
    arrange = lambda v: jnp.take(v.reshape(2, 4, B, 2 * B), which, axis=1).reshape(8 * B, 2 * B)

    own, oth = product(z.astype(jnp.int32).reshape(1), pieces, arrange(full), arrange(alt))
    got = other_core(oth)
    own, got = own.reshape(Z, 1, B, B), got.reshape(Z, 1, B, B)
    half = lax.broadcasted_iota(jnp.int32, (1, 2, 1, 1), 1)
    update = jnp.where(half == k, own, got)
    base = jnp.where(z == 0, 0.0, a.reshape(Z, 2, B, B))
    return (base - update).reshape(16, B, 1, B)


def solution(mesh):
    fine = Mesh(mesh.devices.reshape(Z, X, K, Y), ("z", "x", "k", "y"))
    spec = P(None, "y", None, ("z", "x", "k"))
    return jax.shard_map(shards, mesh=fine, in_specs=(spec, P()), out_specs=spec, check_vma=False)
```

```python
import jax
import jax.numpy as jnp
from jax import lax
from jax.experimental import pallas as pl
from jax.experimental.pallas import tpu as pltpu
from jax.sharding import Mesh
from jax.sharding import PartitionSpec as P

Z, X, K, Y = 8, 4, 2, 4
B = 128
FIRST = (0, 2, 1, 3)
SECOND = (1, 3, 0, 2)


def shift(v, axis, size, step):
    return lax.ppermute(v, axis, [(i, (i + step) % size) for i in range(size)])


def other_core(v):
    return lax.ppermute(v, "k", [(0, 1), (1, 0)])


def swap(v, choice):
    perm = []
    for x in range(X):
        for k in range(K):
            for y in range(Y):
                source = ((2 * k + (y >> 1)) * K + (y & 1)) * Y + choice[x]
                perm.append((source, (x * K + k) * Y + y))
    return lax.ppermute(v, ("x", "k", "y"), perm)


def after(value, *done):
    return lax.optimization_barrier((value, *done))[0]


def after2(values, *done):
    return lax.optimization_barrier((*values, *done))[: len(values)]


def gather_y(v):
    return [v] + [shift(v, "y", Y, s) for s in range(1, Y)]


def split(v):
    high = v.astype(jnp.bfloat16)
    return high, (v - high.astype(jnp.float32)).astype(jnp.bfloat16)


def mul(a, b, transposed):
    dims = (((1,), (1 if transposed else 0,)), ((), ()))
    f = lambda u, v: lax.dot_general(u, v, dims, preferred_element_type=jnp.float32)
    return f(a[0], b[0]) + (f(a[0], b[1]) + f(a[1], b[0]))


VMEM = pl.BlockSpec(memory_space=pltpu.VMEM)
SMEM = pl.BlockSpec(memory_space=pltpu.SMEM)


def at_block(i, n=1):
    return pl.ds(pl.multiple_of(i * B, B), n * B)


def factor(pos, inverse, mine, theirs, corner):
    def body(pos_ref, l_ref, m0, m1, m2, m3, th, c0, c1, c2, c3, fh, fl, ah, al, xc, gs, zz, vv):
        z, x, k, y = (pos_ref[i] for i in range(4))
        low = x < 2
        for s, (m, c) in enumerate(zip((m0, m1, m2, m3), (c0, c1, c2, c3))):
            from_y = lax.rem(y + (Y - s), Y)
            for p in range(2):
                lanes = at_block(4 * p + from_y)
                xc[:B, lanes] = m[p]
                xc[B:, lanes] = th[s, p]
            for i in range(4):
                gs[at_block(jnp.where(low, i, from_y)), at_block(jnp.where(low, from_y, i))] = c[i]
        l0, l1, g = split(l_ref[0]), split(l_ref[1]), split(gs[...])
        row = lax.broadcasted_iota(jnp.int32, (2 * B, 4 * B), 0)
        col = lax.broadcasted_iota(jnp.int32, (2 * B, 4 * B), 1)
        block = 2 * (x & 1) + jnp.where(row < B, k, 1 - k)
        unit = jnp.where(col == block * B + (row & (B - 1)), 1.0, 0.0)
        w = mul(split(xc[:, : 4 * B]), l0, True)
        v = mul(split(w), l0, False)
        u = mul(split(xc[:, 4 * B :] - mul(split(v), g, False)), l1, True)
        corner_slab = z == 0
        w = jnp.where(corner_slab, jnp.where(low, unit, 0.0), w)
        u = jnp.where(corner_slab, jnp.where(low, 0.0, unit), u)
        zb = mul(split(u), l1, False)
        zt = mul(split(w - mul(split(mul(split(zb), g, True)), l0, True)), l0, False)
        sign = jnp.where(corner_slab, -1.0, 1.0)
        zz[:, : 4 * B] = zt * sign
        zz[:, 4 * B :] = zb * sign
        vv[:, : 4 * B] = jnp.where(
            corner_slab,
            jnp.where((k == 1) | low, zt * sign, 0.0),
            jnp.where(k == 1, v, 0.0),
        )
        vv[:, 4 * B :] = jnp.where(corner_slab & ((k == 1) | low), zb * sign, 0.0)
        pick = lambda table, i: jnp.where(i == 0, table[0], jnp.where(i == 1, table[1], jnp.where(i == 2, table[2], table[3])))
        which = (pick(FIRST, x), pick(SECOND, x), pick(FIRST, (x + 3) & 3), pick(FIRST, (x + 1) & 3))
        for p in range(2):
            for j in range(4):
                lanes = slice((4 * p + j) * B, (4 * p + j + 1) * B)
                fh[:, lanes], fl[:, lanes] = split(zz[:, at_block(4 * p + which[j])])
                ah[:, lanes], al[:, lanes] = split(vv[:, at_block(4 * p + which[j])])

    half = jax.ShapeDtypeStruct((2 * B, 8 * B), jnp.bfloat16)
    return pl.pallas_call(
        body,
        out_shape=(half,) * 4,
        in_specs=[SMEM] + [VMEM] * 10,
        out_specs=(VMEM,) * 4,
        scratch_shapes=[
            pltpu.VMEM((2 * B, 8 * B), jnp.float32),
            pltpu.VMEM((4 * B, 4 * B), jnp.float32),
            pltpu.VMEM((2 * B, 8 * B), jnp.float32),
            pltpu.VMEM((2 * B, 8 * B), jnp.float32),
        ],
        compiler_params=pltpu.CompilerParams(vmem_limit_bytes=32 * 2**20),
        cost_estimate=pl.CostEstimate(flops=8 * 3 * 2 * 512 * 512 * 256, bytes_accessed=6 * 2**20, transcendentals=0),
        name="factor",
    )(pos, inverse, *mine, theirs, *corner)


def product(pos, pieces, zs):
    names = [(t, c) for t in range(Z) for c in range(8)]
    arrays, index = [], {}
    for name in names:
        array, at = pieces[name]
        for i, known in enumerate(arrays):
            if known is array:
                break
        else:
            i = len(arrays)
            arrays.append(array)
        index[name] = (i, at)

    def body(pos_ref, *refs):
        xs = refs[: len(arrays)]
        zh, zl, yh, yl, own, oth, xh, xl = refs[len(arrays) :]
        for t, c in names:
            i, at = index[(t, c)]
            high, low = split(xs[i][at])
            xh[t * B : (t + 1) * B, c * B : (c + 1) * B] = high
            xl[t * B : (t + 1) * B, c * B : (c + 1) * B] = low
        z = pos_ref[0]
        res = mul((xh[...], xl[...]), (zh[...], zl[...]), True)
        for t in range(Z):
            rows = at_block(lax.rem(z + t, Z))
            own[rows, :] = res[t * B : (t + 1) * B, :B]
            oth[rows, :] = res[t * B : (t + 1) * B, B:]
        rows = at_block(lax.rem(Z - z, Z))
        alt = mul((xh[rows, :], xl[rows, :]), (yh[...], yl[...]), True)
        own[:B, :] = alt[:, :B]
        oth[:B, :] = alt[:, B:]

    half = jax.ShapeDtypeStruct((Z * B, B), jnp.float32)
    return pl.pallas_call(
        body,
        out_shape=(half, half),
        in_specs=[SMEM] + [VMEM] * (len(arrays) + 4),
        out_specs=(VMEM, VMEM),
        scratch_shapes=[pltpu.VMEM((Z * B, 8 * B), jnp.bfloat16)] * 2,
        compiler_params=pltpu.CompilerParams(vmem_limit_bytes=32 * 2**20),
        cost_estimate=pl.CostEstimate(flops=2 * 3 * 1024 * 1024 * 256, bytes_accessed=7 * 2**20, transcendentals=0),
        name="product",
    )(pos, *arrays, *zs)


def finish(pos, a, own, got):
    def body(pos_ref, a_ref, own_ref, got_ref, out_ref):
        z, k = pos_ref[0], pos_ref[2]
        for t in range(Z):
            out_ref[2 * t + k] = jnp.where(z == 0, 0.0, a_ref[2 * t + k]) - own_ref[t]
            out_ref[2 * t + 1 - k] = jnp.where(z == 0, 0.0, a_ref[2 * t + 1 - k]) - got_ref[t]

    return pl.pallas_call(
        body,
        out_shape=jax.ShapeDtypeStruct((2 * Z, B, B), jnp.float32),
        in_specs=[SMEM] + [VMEM] * 3,
        out_specs=VMEM,
        compiler_params=pltpu.CompilerParams(vmem_limit_bytes=16 * 2**20),
        cost_estimate=pl.CostEstimate(flops=2**18, bytes_accessed=3 * 2**20, transcendentals=0),
        name="finish",
    )(pos, a, own.reshape(Z, B, B), got.reshape(Z, B, B))


def shards(matrix, inverse_factors):
    z, x, k, y = (lax.axis_index(n) for n in ("z", "x", "k", "y"))
    pos = jnp.stack([z, x, k, y]).astype(jnp.int32)
    a = matrix.reshape(16, B, B)

    blocks = jnp.swapaxes(a[:2], 1, 2)
    f0, g0 = swap(blocks, FIRST), swap(blocks, SECOND)

    def step(u, d):
        return shift(u, "z", Z, 1), shift(d, "z", Z, -1)

    def last(u, d):
        return shift(u[:1], "z", Z, 1), shift(d[1:], "z", Z, -1)

    def along_x(*parts):
        v = jnp.concatenate(parts)
        return shift(v, "x", X, 1), shift(v, "x", X, -1)

    corner = jnp.where(x < 2, blocks[1], a[0])

    def spread(v, reach):
        got = lax.ppermute(v, "z", [(i, i + reach) for i in range(0, Z, 2 * reach)])
        return jnp.where(z % (2 * reach) == reach, got, v)

    corner = spread(corner, 4)
    f1u, f1d = step(f0, f0)
    g1u, g1d = step(g0, g0)
    corner = spread(after(corner, f0), 2)
    rows = gather_y(after(blocks, f0))
    f2u, f2d = step(*after2((f1u, f1d), corner))
    x0 = along_x(f0, f1u, f1d)
    corner = spread(corner, 1)
    g2u, g2d = step(g1u, g1d)
    f3u, f3d = step(*after2((f2u, f2d), corner))
    got = other_core(corner)
    corner = jnp.stack([jnp.where(k == 0, corner, got), jnp.where(k == 0, got, corner)])
    got = lax.ppermute(corner, "x", [(0, 1), (1, 0), (2, 3), (3, 2)])
    corner = jnp.stack([jnp.where(x % 2 == 0, corner, got), jnp.where(x % 2 == 0, got, corner)]).reshape(4, B, B)
    x1 = along_x(*after2((f2u, f2d), *x0))
    g3u, g3d = step(*after2((g2u, g2d), *x0))
    fa, fb = last(*after2((f3u, f3d), corner))
    corners = gather_y(corner)
    ga, gb = last(*after2((g3u, g3d), *x1))
    x2 = along_x(f3u, f3d, fa, fb)
    theirs = other_core(jnp.stack(rows))

    pieces = {}
    first = {0: f0, 1: f1d, 2: f2d, 3: f3d, 5: f3u, 6: f2u, 7: f1u}
    second = {0: g0, 1: g1d, 2: g2d, 3: g3d, 5: g3u, 6: g2u, 7: g1u}
    beside = {0: (x0, 0), 7: (x0, 2), 1: (x0, 4), 6: (x1, 0), 2: (x1, 2), 5: (x2, 0), 3: (x2, 2), 4: (x2, 4)}
    for t in range(Z):
        for p in range(2):
            pieces[(t, 4 * p)] = ((fa, fb)[p], 0) if t == 4 else (first[t], p)
            pieces[(t, 4 * p + 1)] = ((ga, gb)[p], 0) if t == 4 else (second[t], p)
            arrived, at = beside[t]
            pieces[(t, 4 * p + 2)] = (arrived[0], at + p)
            pieces[(t, 4 * p + 3)] = (arrived[1], at + p)

    zs = factor(pos, inverse_factors, rows, theirs, corners)
    own, other = product(pos, pieces, zs)
    return finish(pos, a, own, other_core(other)).reshape(16, B, 1, B)


def solution(mesh):
    fine = Mesh(mesh.devices.reshape(Z, X, K, Y), ("z", "x", "k", "y"))
    spec = P(None, "y", None, ("z", "x", "k"))
    return jax.shard_map(shards, mesh=fine, in_specs=(spec, P()), out_specs=spec, check_vma=False)
```

```python
import jax
import jax.numpy as jnp
from jax import lax
from jax.experimental import pallas as pl
from jax.experimental.pallas import tpu as pltpu
from jax.sharding import Mesh
from jax.sharding import PartitionSpec as P

Z, X, K, Y = 8, 4, 2, 4
B = 128
FIRST = (0, 2, 1, 3)
SECOND = (1, 3, 0, 2)


def shift(v, axis, size, step):
    return lax.ppermute(v, axis, [(i, (i + step) % size) for i in range(size)])


def other_core(v):
    return lax.ppermute(v, "k", [(0, 1), (1, 0)])


def swap(v, choice):
    perm = []
    for x in range(X):
        for k in range(K):
            for y in range(Y):
                source = ((2 * k + (y >> 1)) * K + (y & 1)) * Y + choice[x]
                perm.append((source, (x * K + k) * Y + y))
    return lax.ppermute(v, ("x", "k", "y"), perm)


def after(value, *done):
    return lax.optimization_barrier((value, *done))[0]


def gather_y(v):
    return [v] + [shift(v, "y", Y, s) for s in range(1, Y)]


def split(v):
    high = v.astype(jnp.bfloat16)
    return high, (v - high.astype(jnp.float32)).astype(jnp.bfloat16)


def mul(a, b, transposed):
    dims = (((1,), (1 if transposed else 0,)), ((), ()))
    f = lambda u, v: lax.dot_general(u, v, dims, preferred_element_type=jnp.float32)
    return f(a[0], b[0]) + (f(a[0], b[1]) + f(a[1], b[0]))


VMEM = pl.BlockSpec(memory_space=pltpu.VMEM)
SMEM = pl.BlockSpec(memory_space=pltpu.SMEM)


def at_block(i, n=1):
    return pl.ds(pl.multiple_of(i * B, B), n * B)


def pick(table, i):
    return jnp.where(i == 0, table[0], jnp.where(i == 1, table[1], jnp.where(i == 2, table[2], table[3])))


def params(mib):
    return pltpu.CompilerParams(vmem_limit_bytes=mib * 2**20)


def cost(products, mib):
    return pl.CostEstimate(flops=int(products * 6 * 512 * 512 * 256), bytes_accessed=mib * 2**20, transcendentals=0)


WIDE = jax.ShapeDtypeStruct((2 * B, 4 * B), jnp.float32)
WIDE16 = jax.ShapeDtypeStruct((2 * B, 4 * B), jnp.bfloat16)
SQUARE16 = jax.ShapeDtypeStruct((4 * B, 4 * B), jnp.bfloat16)
Z16 = jax.ShapeDtypeStruct((2 * B, 8 * B), jnp.bfloat16)


def first_panel(pos, inverse, mine, theirs):
    def body(pos_ref, l_ref, m0, m1, m2, m3, th, w_ref, vh, vl, x1, l0h, l0l, l1h, l1l, xc):
        y = pos_ref[3]
        for s, m in enumerate((m0, m1, m2, m3)):
            lanes = at_block(lax.rem(y + (Y - s), Y))
            xc[:B, lanes] = m[0]
            xc[B:, lanes] = th[s, 0]
            x1[:B, lanes] = m[1]
            x1[B:, lanes] = th[s, 1]
        l0 = l0h[...], l0l[...] = split(l_ref[0])
        l1h[...], l1l[...] = split(l_ref[1])
        w = mul(split(xc[...]), l0, True)
        w_ref[...] = w
        vh[...], vl[...] = split(mul(split(w), l0, False))

    return pl.pallas_call(
        body,
        out_shape=(WIDE, WIDE16, WIDE16, WIDE) + (SQUARE16,) * 4,
        in_specs=[SMEM] + [VMEM] * 6,
        out_specs=(VMEM,) * 8,
        scratch_shapes=[pltpu.VMEM((2 * B, 4 * B), jnp.float32)],
        compiler_params=params(24),
        cost_estimate=cost(2, 7),
        name="first_panel",
    )(pos, inverse, *mine, theirs)


def second_panel(pos, panel, corner):
    def body(pos_ref, w_ref, vh, vl, x1, l0h, l0l, l1h, l1l, c0, c1, c2, c3, fh, fl, ah, al, gs, vg, bg, zz):
        z, x, k, y = (pos_ref[i] for i in range(4))
        for s, c in enumerate((c0, c1, c2, c3)):
            rows = at_block(lax.rem(y + (Y - s), Y))
            for i in range(4):
                table = (FIRST, SECOND)[i % 2]
                gs[rows, at_block(pick(table, x ^ 1 if i >= 2 else x))] = c[i]
        l0, l1, v, g = (l0h[...], l0l[...]), (l1h[...], l1l[...]), (vh[...], vl[...]), split(gs[...])

        @pl.when(k == 0)
        def _():
            vg[...] = mul(v, g, False)

        @pl.when(k == 1)
        def _():
            vg[...] = mul(v, g, True)

        row = lax.broadcasted_iota(jnp.int32, (2 * B, 4 * B), 0)
        col = lax.broadcasted_iota(jnp.int32, (2 * B, 4 * B), 1)
        block = 2 * (x & 1) + jnp.where(row < B, k, 1 - k)
        unit = jnp.where(col == block * B + (row & (B - 1)), 1.0, 0.0)
        corner_slab, low = z == 0, x < 2
        u = mul(split(x1[...] - vg[...]), l1, True)
        w = jnp.where(corner_slab, jnp.where(low, unit, 0.0), w_ref[...])
        u = jnp.where(corner_slab, jnp.where(low, 0.0, unit), u)
        zb = mul(split(u), l1, False)

        @pl.when(k == 0)
        def _():
            bg[...] = mul(split(zb), g, True)

        @pl.when(k == 1)
        def _():
            bg[...] = mul(split(zb), g, False)

        zt = mul(split(w - mul(split(bg[...]), l0, True)), l0, False)
        sign = jnp.where(corner_slab, -1.0, 1.0)
        zz[:, : 4 * B] = zt * sign
        zz[:, 4 * B :] = zb * sign
        beside = (x + jnp.where(k == 0, 3, 1)) & 3
        which = (pick(FIRST, x), pick(SECOND, x), pick(FIRST, beside), pick(SECOND, beside))
        for j in range(4):
            lanes = slice(j * B, (j + 1) * B)
            ah[:, lanes] = vh[:, at_block(which[j])]
            al[:, lanes] = vl[:, at_block(which[j])]
            for p in range(2):
                lanes = slice((4 * p + j) * B, (4 * p + j + 1) * B)
                fh[:, lanes], fl[:, lanes] = split(zz[:, at_block(4 * p + which[j])])

    return pl.pallas_call(
        body,
        out_shape=(Z16, Z16, WIDE16, WIDE16),
        in_specs=[SMEM] + [VMEM] * 12,
        out_specs=(VMEM,) * 4,
        scratch_shapes=[
            pltpu.VMEM((4 * B, 4 * B), jnp.float32),
            pltpu.VMEM((2 * B, 4 * B), jnp.float32),
            pltpu.VMEM((2 * B, 4 * B), jnp.float32),
            pltpu.VMEM((2 * B, 8 * B), jnp.float32),
        ],
        compiler_params=params(24),
        cost_estimate=cost(6, 6),
        name="second_panel",
    )(pos, *panel, *corner)


SLOTS = [(0, None)] + [(t, h) for t in (1, 2, 3) for h in (0, 1)] + [(4, None)]


def row_block(z, k, slot):
    t, h = SLOTS[slot]
    return 2 * lax.rem(z + jnp.where(k == 0, Z - t, t), Z) + (k if h is None else h)


def product(pos, pieces, zs):
    arrays, index = [], {}
    for i in range(8):
        for c in range(8):
            array, *at = pieces[i][c]
            for n, known in enumerate(arrays):
                if known is array:
                    break
            else:
                n = len(arrays)
                arrays.append(array)
            index[(i, c)] = (n, tuple(at))

    def body(pos_ref, *refs):
        xs = refs[: len(arrays)]
        zh, zl, ah, al, own, oth, xh, xl = refs[len(arrays) :]
        z, x, k = pos_ref[0], pos_ref[1], pos_ref[2]
        for (i, c), (n, at) in index.items():
            high, low = split(xs[n][at])
            xh[i * B : (i + 1) * B, c * B : (c + 1) * B] = high
            xl[i * B : (i + 1) * B, c * B : (c + 1) * B] = low
        res = mul((xh[...], xl[...]), (zh[...], zl[...]), True)
        own[...] = res[:, :B]
        oth[...] = res[:, B:]
        for i in range(8):
            block = row_block(z, k, i)
            rows = slice(i * B, (i + 1) * B)

            @pl.when((block == 0) & ((z != 0) | (x >= 2)))
            def _():
                own[rows, :] = jnp.zeros((B, B), jnp.float32)
                oth[rows, :] = jnp.zeros((B, B), jnp.float32)

            @pl.when((block == 1) & (z != 0))
            def _():
                part = mul((xh[rows, : 4 * B], xl[rows, : 4 * B]), (ah[...], al[...]), True)
                own[rows, :] = part[:, :B]
                oth[rows, :] = part[:, B:]

    half = jax.ShapeDtypeStruct((8 * B, B), jnp.float32)
    return pl.pallas_call(
        body,
        out_shape=(half, half),
        in_specs=[SMEM] + [VMEM] * (len(arrays) + 4),
        out_specs=(VMEM, VMEM),
        scratch_shapes=[pltpu.VMEM((8 * B, 8 * B), jnp.bfloat16)] * 2,
        compiler_params=params(32),
        cost_estimate=cost(8, 7),
        name="product",
    )(pos, *arrays, *zs)


def finish(pos, a, own, got):
    def body(pos_ref, a_ref, own_ref, got_ref, out_ref):
        z, k = pos_ref[0], pos_ref[2]
        for i in range(8):
            for core, ref in ((k, own_ref), (1 - k, got_ref)):
                block = row_block(z, core, i)
                out_ref[block] = jnp.where(z == 0, 0.0, a_ref[block]) - ref[i]

    return pl.pallas_call(
        body,
        out_shape=jax.ShapeDtypeStruct((2 * Z, B, B), jnp.float32),
        in_specs=[SMEM] + [VMEM] * 3,
        out_specs=VMEM,
        compiler_params=params(16),
        cost_estimate=cost(0, 3),
        name="finish",
    )(pos, a, own.reshape(Z, B, B), got.reshape(Z, B, B))


def shards(matrix, inverse_factors):
    z, x, k, y = (lax.axis_index(n) for n in ("z", "x", "k", "y"))
    pos = jnp.stack([z, x, k, y]).astype(jnp.int32)
    a = matrix.reshape(16, B, B)

    def around(v, axis, size):
        perm = [(2 * i, 2 * ((i + 1) % size)) for i in range(size)]
        perm += [(2 * i + 1, 2 * ((i - 1) % size) + 1) for i in range(size)]
        return lax.ppermute(v, (axis, "k"), perm)

    blocks = jnp.swapaxes(a[:2], 1, 2)
    fg = jnp.stack([swap(blocks, FIRST), swap(blocks, SECOND)])
    got = other_core(fg)
    slab = jnp.stack([jnp.where(k == 0, fg, got), jnp.where(k == 0, got, fg)])
    rows = gather_y(after(blocks, fg))

    corner = jnp.where(k == 0, fg[:, 1], fg[:, 0])

    def spread(v, reach):
        got = lax.ppermute(v, "z", [(i, i + reach) for i in range(0, Z, 2 * reach)])
        return jnp.where(z % (2 * reach) == reach, got, v)

    s0 = around(fg, "x", X)
    r1 = around(slab, "z", Z)
    corner = spread(after(corner, slab), 4)
    s1 = around(r1, "x", X)
    r2 = around(after(r1, s0, corner), "z", Z)
    corner = spread(corner, 2)
    theirs = other_core(jnp.stack(rows))
    s2 = around(after(r2, s1), "x", X)
    r3 = around(after(r2, s1, corner), "z", Z)
    panel = first_panel(pos, inverse_factors, rows, theirs)
    corner = spread(corner, 1)
    half = lax.dynamic_index_in_dim(after(r3, s2, corner), k, 0, keepdims=False)
    r4 = around(half, "z", Z)
    s3 = around(after(r3, s2), "x", X)
    got = lax.ppermute(corner, "x", [(0, 1), (1, 0), (2, 3), (3, 2)])
    corners = gather_y(jnp.concatenate([corner, got]))
    s4 = around(r4, "x", X)

    def piece(ring, side, *at):
        return [((ring, side)[j // 2], *at, j % 2, p) for p in range(2) for j in range(4)]

    pieces = [piece(fg, s0)]
    for ring, side in ((r1, s1), (r2, s2), (r3, s3)):
        pieces += [piece(ring, side, 0), piece(ring, side, 1)]
    pieces += [piece(r4, s4)]

    zs = second_panel(pos, panel, corners)
    own, other = product(pos, pieces, zs)
    return finish(pos, a, own, other_core(other)).reshape(16, B, 1, B)


def solution(mesh):
    fine = Mesh(mesh.devices.reshape(Z, X, K, Y), ("z", "x", "k", "y"))
    spec = P(None, "y", None, ("z", "x", "k"))
    return jax.shard_map(shards, mesh=fine, in_specs=(spec, P()), out_specs=spec, check_vma=False)
```

```python
import jax
import jax.numpy as jnp
from jax import lax
from jax.experimental import pallas as pl
from jax.experimental.pallas import tpu as pltpu
from jax.sharding import Mesh
from jax.sharding import PartitionSpec as P

Z, X, K, Y = 8, 4, 2, 4
B = 128
FIRST = (0, 2, 1, 3)
SECOND = (1, 3, 0, 2)


def shift(v, axis, size, step):
    return lax.ppermute(v, axis, [(i, (i + step) % size) for i in range(size)])


def other_core(v):
    return lax.ppermute(v, "k", [(0, 1), (1, 0)])


def swap(v, choice):
    perm = []
    for x in range(X):
        for k in range(K):
            for y in range(Y):
                source = ((2 * k + (y >> 1)) * K + (y & 1)) * Y + choice[x]
                perm.append((source, (x * K + k) * Y + y))
    return lax.ppermute(v, ("x", "k", "y"), perm)


def after(value, *done):
    return lax.optimization_barrier((value, *done))[0]


def gather_y(v):
    return [v] + [shift(v, "y", Y, s) for s in range(1, Y)]


def split(v):
    high = v.astype(jnp.bfloat16)
    return high, (v - high.astype(jnp.float32)).astype(jnp.bfloat16)


def mul(a, b, transposed):
    dims = (((1,), (1 if transposed else 0,)), ((), ()))
    f = lambda u, v: lax.dot_general(u, v, dims, preferred_element_type=jnp.float32)
    return f(a[0], b[0]) + (f(a[0], b[1]) + f(a[1], b[0]))


VMEM = pl.BlockSpec(memory_space=pltpu.VMEM)
SMEM = pl.BlockSpec(memory_space=pltpu.SMEM)


def at_block(i, n=1):
    return pl.ds(pl.multiple_of(i * B, B), n * B)


def pick(table, i):
    return jnp.where(i == 0, table[0], jnp.where(i == 1, table[1], jnp.where(i == 2, table[2], table[3])))


def params(mib):
    return pltpu.CompilerParams(vmem_limit_bytes=mib * 2**20)


def cost(products, mib):
    return pl.CostEstimate(flops=int(products * 6 * 512 * 512 * 256), bytes_accessed=mib * 2**20, transcendentals=0)


WIDE16 = jax.ShapeDtypeStruct((2 * B, 4 * B), jnp.bfloat16)
Z16 = jax.ShapeDtypeStruct((2 * B, 8 * B), jnp.bfloat16)


def factor(pos, inverse, gathered, got):
    def body(pos_ref, l_ref, q0, q1, q2, q3, got_ref, fh, fl, ah, al, xc, gs, vg, bg, zz):
        z, x, k, y = (pos_ref[i] for i in range(4))
        corner_slab, low = z == 0, x < 2

        def place(rows, corner):
            for s in range(Y):
                from_y = lax.rem(y + (Y - s), Y)
                for p in range(2):
                    lanes = at_block(4 * p + from_y)
                    xc[:B, lanes] = rows(s, 2 * k + p)
                    xc[B:, lanes] = rows(s, 2 * (1 - k) + p)
                for i in range(4):
                    m = 2 * ((x + i // 2) & 1) + i % 2
                    gs[at_block(m), at_block(from_y)] = corner(s, i)

        mine = (q0, q1, q2, q3)

        @pl.when(k == 0)
        def _():
            place(lambda s, i: mine[s][i], lambda s, i: got_ref[s, i])

        @pl.when(k == 1)
        def _():
            place(lambda s, i: got_ref[s, i], lambda s, i: mine[s][i])

        l0, l1, g = split(l_ref[0]), split(l_ref[1]), split(gs[...])
        w = mul(split(xc[:, : 4 * B]), l0, True)
        v = split(mul(split(w), l0, False))

        @pl.when(low)
        def _():
            vg[...] = mul(v, g, False)

        @pl.when(x >= 2)
        def _():
            vg[...] = mul(v, g, True)

        row = lax.broadcasted_iota(jnp.int32, (2 * B, 4 * B), 0)
        col = lax.broadcasted_iota(jnp.int32, (2 * B, 4 * B), 1)
        block = 2 * (x & 1) + jnp.where(row < B, k, 1 - k)
        unit = jnp.where(col == block * B + (row & (B - 1)), 1.0, 0.0)
        u = mul(split(xc[:, 4 * B :] - vg[...]), l1, True)
        w = jnp.where(corner_slab, jnp.where(low, unit, 0.0), w)
        u = jnp.where(corner_slab, jnp.where(low, 0.0, unit), u)
        zb = mul(split(u), l1, False)

        @pl.when(low)
        def _():
            bg[...] = mul(split(zb), g, True)

        @pl.when(x >= 2)
        def _():
            bg[...] = mul(split(zb), g, False)

        zt = mul(split(w - mul(split(bg[...]), l0, True)), l0, False)
        sign = jnp.where(corner_slab, -1.0, 1.0)
        zz[:, : 4 * B] = zt * sign
        zz[:, 4 * B :] = zb * sign
        vg[...] = v[0].astype(jnp.float32)
        bg[...] = v[1].astype(jnp.float32)
        beside = (x + jnp.where(k == 0, 3, 1)) & 3
        which = (pick(FIRST, x), pick(SECOND, x), pick(FIRST, beside), pick(SECOND, beside))
        for j in range(4):
            lanes = slice(j * B, (j + 1) * B)
            ah[:, lanes] = vg[:, at_block(which[j])].astype(jnp.bfloat16)
            al[:, lanes] = bg[:, at_block(which[j])].astype(jnp.bfloat16)
            for p in range(2):
                lanes = slice((4 * p + j) * B, (4 * p + j + 1) * B)
                fh[:, lanes], fl[:, lanes] = split(zz[:, at_block(4 * p + which[j])])

    wide = pltpu.VMEM((2 * B, 4 * B), jnp.float32)
    return pl.pallas_call(
        body,
        out_shape=(Z16, Z16, WIDE16, WIDE16),
        in_specs=[SMEM] + [VMEM] * 6,
        out_specs=(VMEM,) * 4,
        scratch_shapes=[
            pltpu.VMEM((2 * B, 8 * B), jnp.float32),
            pltpu.VMEM((4 * B, 4 * B), jnp.float32),
            wide,
            wide,
            pltpu.VMEM((2 * B, 8 * B), jnp.float32),
        ],
        compiler_params=params(20),
        cost_estimate=cost(8, 6),
        name="factor",
    )(pos, inverse, *gathered, got)


SLOTS = [(0, 0)] + [(t, h) for t in (1, 2, 3) for h in (0, 1)] + [(4, 0)]


def row_block(z, k, slot):
    t, h = SLOTS[slot]
    return 2 * lax.rem(z + jnp.where(k == 0, Z - t, t), Z) + (k if h == 0 else 1 - k)


def product(pos, pieces, zs):
    arrays, index = [], {}
    for i in range(8):
        for c in range(8):
            array, *at = pieces[i][c]
            for n, known in enumerate(arrays):
                if known is array:
                    break
            else:
                n = len(arrays)
                arrays.append(array)
            index[(i, c)] = (n, tuple(at))

    def body(pos_ref, *refs):
        xs = refs[: len(arrays)]
        zh, zl, ah, al, own, oth, xh, xl = refs[len(arrays) :]
        z, x, k = pos_ref[0], pos_ref[1], pos_ref[2]
        for (i, c), (n, at) in index.items():
            high, low = split(xs[n][at])
            xh[i * B : (i + 1) * B, c * B : (c + 1) * B] = high
            xl[i * B : (i + 1) * B, c * B : (c + 1) * B] = low
        res = mul((xh[...], xl[...]), (zh[...], zl[...]), True)
        own[...] = res[:, :B]
        oth[...] = res[:, B:]
        for i in range(8):
            block = row_block(z, k, i)
            rows = slice(i * B, (i + 1) * B)

            @pl.when((block == 0) & ((z != 0) | (x >= 2)))
            def _():
                own[rows, :] = jnp.zeros((B, B), jnp.float32)
                oth[rows, :] = jnp.zeros((B, B), jnp.float32)

            @pl.when((block == 1) & (z != 0))
            def _():
                part = mul((xh[rows, : 4 * B], xl[rows, : 4 * B]), (ah[...], al[...]), True)
                own[rows, :] = part[:, :B]
                oth[rows, :] = part[:, B:]

    half = jax.ShapeDtypeStruct((8 * B, B), jnp.float32)
    return pl.pallas_call(
        body,
        out_shape=(half, half),
        in_specs=[SMEM] + [VMEM] * (len(arrays) + 4),
        out_specs=(VMEM, VMEM),
        scratch_shapes=[pltpu.VMEM((8 * B, 8 * B), jnp.bfloat16)] * 2,
        compiler_params=params(20),
        cost_estimate=cost(8, 7),
        name="product",
    )(pos, *arrays, *zs)


def finish(pos, a, own, got):
    def body(pos_ref, a_ref, own_ref, got_ref, out_ref):
        z, k = pos_ref[0], pos_ref[2]
        for i in range(8):
            for core, ref in ((k, own_ref), (1 - k, got_ref)):
                block = row_block(z, core, i)
                out_ref[block] = jnp.where(z == 0, 0.0, a_ref[block]) - ref[i]

    return pl.pallas_call(
        body,
        out_shape=jax.ShapeDtypeStruct((2 * Z, B, B), jnp.float32),
        in_specs=[SMEM] + [VMEM] * 3,
        out_specs=VMEM,
        compiler_params=params(8),
        cost_estimate=cost(0, 3),
        name="finish",
    )(pos, a, own.reshape(Z, B, B), got.reshape(Z, B, B))


def shards(matrix, inverse_factors):
    z, x, k, y = (lax.axis_index(n) for n in ("z", "x", "k", "y"))
    pos = jnp.stack([z, x, k, y]).astype(jnp.int32)
    a = matrix.reshape(16, B, B)

    def around(v, axis, size):
        perm = [(2 * i, 2 * ((i + 1) % size)) for i in range(size)]
        perm += [(2 * i + 1, 2 * ((i - 1) % size) + 1) for i in range(size)]
        return lax.ppermute(v, (axis, "k"), perm)

    blocks = jnp.swapaxes(a[:2], 1, 2)
    f0, g0 = swap(blocks, FIRST), swap(blocks, SECOND)

    theirs = other_core(blocks)
    columns = jnp.where(k == 0, jnp.concatenate([blocks, theirs]), jnp.concatenate([theirs, blocks]))
    corner = jnp.where(x < 2, columns[1::2], columns[::2])

    def to_core1(v, pairs):
        return lax.ppermute(v, ("z", "k"), [(2 * i + c, 2 * j + 1) for i, c, j in pairs])

    near, far = to_core1(corner, [(0, 0, 4), (0, 1, 2)]), to_core1(corner, [(0, 0, 6)])
    fg = jnp.stack([f0, g0])
    slab = jnp.stack([fg, other_core(fg)])
    r1 = around(slab, "z", Z)
    s0 = around(fg, "x", X)
    corner = jnp.where((z == 4) | (z == 2), near, jnp.where(z == 6, far, corner))
    corner = jnp.where(z % 2 == 1, to_core1(corner, [(0, 0, 1), (2, 1, 3), (4, 1, 5), (6, 1, 7)]), corner)
    beside = lax.ppermute(corner, ("x", "k"), [(2 * i + 1, 2 * (i ^ 1) + 1) for i in range(X)])
    gathered = gather_y(jnp.where(k == 0, columns, jnp.concatenate([corner, beside])))

    r2 = around(after(r1, s0), "z", Z)
    s1 = around(after(r1, s0), "x", X)
    r3 = around(after(r2, s1, gathered[0]), "z", Z)
    s2 = around(after(r2, s1, gathered[0]), "x", X)
    zs = factor(pos, inverse_factors, gathered, other_core(jnp.stack(gathered)))
    r4 = around(after(r3[0], s2), "z", Z)
    s3 = around(after(r3, s2), "x", X)
    s4 = around(after(r4, *zs), "x", X)

    def piece(ring, side, *at):
        return [((ring, side)[j // 2], *at, j % 2, p) for p in range(2) for j in range(4)]

    pieces = [piece(fg, s0)]
    for ring, side in ((r1, s1), (r2, s2), (r3, s3)):
        pieces += [piece(ring, side, 0), piece(ring, side, 1)]
    pieces += [piece(r4, s4)]

    own, other = product(pos, pieces, zs)
    return finish(pos, a, own, other_core(other)).reshape(16, B, 1, B)


def solution(mesh):
    fine = Mesh(mesh.devices.reshape(Z, X, K, Y), ("z", "x", "k", "y"))
    spec = P(None, "y", None, ("z", "x", "k"))
    return jax.shard_map(shards, mesh=fine, in_specs=(spec, P()), out_specs=spec, check_vma=False)
```

```python
import jax
import jax.numpy as jnp
from jax import lax
from jax.experimental import pallas as pl
from jax.experimental.pallas import tpu as pltpu
from jax.sharding import Mesh
from jax.sharding import PartitionSpec as P

Z, X, K, Y = 8, 4, 2, 4
B = 128
FIRST = (0, 2, 1, 3)
SECOND = (1, 3, 0, 2)


def shift(v, axis, size, step):
    return lax.ppermute(v, axis, [(i, (i + step) % size) for i in range(size)])


def other_core(v):
    return lax.ppermute(v, "k", [(0, 1), (1, 0)])


def swap(v, choice):
    perm = []
    for x in range(X):
        for k in range(K):
            for y in range(Y):
                source = ((2 * k + (y >> 1)) * K + (y & 1)) * Y + choice[x]
                perm.append((source, (x * K + k) * Y + y))
    return lax.ppermute(v, ("x", "k", "y"), perm)


def after(value, *done):
    return lax.optimization_barrier((value, *done))[0]


def gather_y(v):
    return [v] + [shift(v, "y", Y, s) for s in range(1, Y)]


def split(v):
    high = v.astype(jnp.bfloat16)
    return high, (v - high.astype(jnp.float32)).astype(jnp.bfloat16)


def mul(a, b, transposed):
    dims = (((1,), (1 if transposed else 0,)), ((), ()))
    f = lambda u, v: lax.dot_general(u, v, dims, preferred_element_type=jnp.float32)
    return f(a[0], b[0]) + (f(a[0], b[1]) + f(a[1], b[0]))


VMEM = pl.BlockSpec(memory_space=pltpu.VMEM)
SMEM = pl.BlockSpec(memory_space=pltpu.SMEM)


def at_block(i, n=1):
    return pl.ds(pl.multiple_of(i * B, B), n * B)


def pick(table, i):
    return jnp.where(i == 0, table[0], jnp.where(i == 1, table[1], jnp.where(i == 2, table[2], table[3])))


def params(mib):
    return pltpu.CompilerParams(vmem_limit_bytes=mib * 2**20)


def cost(products, mib):
    return pl.CostEstimate(flops=int(products * 6 * 512 * 512 * 256), bytes_accessed=mib * 2**20, transcendentals=0)


WIDE16 = jax.ShapeDtypeStruct((2 * B, 4 * B), jnp.bfloat16)
Z16 = jax.ShapeDtypeStruct((2 * B, 8 * B), jnp.bfloat16)


def factor(pos, inverse, gathered, got):
    def body(pos_ref, l_ref, q0, q1, q2, q3, got_ref, fh, fl, ah, al, xc, gs, vg, bg, zz):
        z, x, k, y = (pos_ref[i] for i in range(4))
        corner_slab, low = z == 0, x < 2

        def place(rows, corner):
            for s in range(Y):
                from_y = lax.rem(y + (Y - s), Y)
                for p in range(2):
                    lanes = at_block(4 * p + from_y)
                    xc[:B, lanes] = rows(s, 2 * k + p)
                    xc[B:, lanes] = rows(s, 2 * (1 - k) + p)
                for i in range(4):
                    m = 2 * ((x + i // 2) & 1) + i % 2
                    gs[at_block(m), at_block(from_y)] = corner(s, i)

        mine = (q0, q1, q2, q3)

        @pl.when(k == 0)
        def _():
            place(lambda s, i: mine[s][i], lambda s, i: got_ref[s, i])

        @pl.when(k == 1)
        def _():
            place(lambda s, i: got_ref[s, i], lambda s, i: mine[s][i])

        l0, l1, g = split(l_ref[0]), split(l_ref[1]), split(gs[...])
        w = mul(split(xc[:, : 4 * B]), l0, True)
        v = split(mul(split(w), l0, False))

        @pl.when(low)
        def _():
            vg[...] = mul(v, g, False)

        @pl.when(x >= 2)
        def _():
            vg[...] = mul(v, g, True)

        row = lax.broadcasted_iota(jnp.int32, (2 * B, 4 * B), 0)
        col = lax.broadcasted_iota(jnp.int32, (2 * B, 4 * B), 1)
        block = 2 * (x & 1) + jnp.where(row < B, k, 1 - k)
        unit = jnp.where(col == block * B + (row & (B - 1)), 1.0, 0.0)
        u = mul(split(xc[:, 4 * B :] - vg[...]), l1, True)
        w = jnp.where(corner_slab, jnp.where(low, unit, 0.0), w)
        u = jnp.where(corner_slab, jnp.where(low, 0.0, unit), u)
        zb = mul(split(u), l1, False)

        @pl.when(low)
        def _():
            bg[...] = mul(split(zb), g, True)

        @pl.when(x >= 2)
        def _():
            bg[...] = mul(split(zb), g, False)

        zt = mul(split(w - mul(split(bg[...]), l0, True)), l0, False)
        sign = jnp.where(corner_slab, -1.0, 1.0)
        zz[:, : 4 * B] = zt * sign
        zz[:, 4 * B :] = zb * sign
        vg[...] = v[0].astype(jnp.float32)
        bg[...] = v[1].astype(jnp.float32)
        beside = (x + jnp.where(k == 0, 3, 1)) & 3
        which = (pick(FIRST, x), pick(SECOND, x), pick(FIRST, beside), pick(SECOND, beside))
        for j in range(4):
            lanes = slice(j * B, (j + 1) * B)
            ah[:, lanes] = vg[:, at_block(which[j])].astype(jnp.bfloat16)
            al[:, lanes] = bg[:, at_block(which[j])].astype(jnp.bfloat16)
            for p in range(2):
                lanes = slice((4 * p + j) * B, (4 * p + j + 1) * B)
                fh[:, lanes], fl[:, lanes] = split(zz[:, at_block(4 * p + which[j])])

    wide = pltpu.VMEM((2 * B, 4 * B), jnp.float32)
    return pl.pallas_call(
        body,
        out_shape=(Z16, Z16, WIDE16, WIDE16),
        in_specs=[SMEM] + [VMEM] * 6,
        out_specs=(VMEM,) * 4,
        scratch_shapes=[
            pltpu.VMEM((2 * B, 8 * B), jnp.float32),
            pltpu.VMEM((4 * B, 4 * B), jnp.float32),
            wide,
            wide,
            pltpu.VMEM((2 * B, 8 * B), jnp.float32),
        ],
        compiler_params=params(20),
        cost_estimate=cost(8, 6),
        name="factor",
    )(pos, inverse, *gathered, got)


SLOTS = [(0, 0)] + [(t, h) for t in (1, 2, 3) for h in (0, 1)] + [(4, 0)]


def row_block(z, k, slot):
    t, h = SLOTS[slot]
    return 2 * lax.rem(z + jnp.where(k == 0, Z - t, t), Z) + (k if h == 0 else 1 - k)


def product(pos, pieces, zs):
    arrays, index = [], {}
    for i in range(8):
        for c in range(8):
            array, *at = pieces[i][c]
            for n, known in enumerate(arrays):
                if known is array:
                    break
            else:
                n = len(arrays)
                arrays.append(array)
            index[(i, c)] = (n, tuple(at))

    def body(pos_ref, *refs):
        xs = refs[: len(arrays)]
        zh, zl, ah, al, own, oth, xh, xl = refs[len(arrays) :]
        z, x, k = pos_ref[0], pos_ref[1], pos_ref[2]
        for (i, c), (n, at) in index.items():
            high, low = split(xs[n][at])
            xh[i * B : (i + 1) * B, c * B : (c + 1) * B] = high
            xl[i * B : (i + 1) * B, c * B : (c + 1) * B] = low
        res = mul((xh[...], xl[...]), (zh[...], zl[...]), True)
        own[...] = res[:, :B]
        oth[...] = res[:, B:]
        for i in range(8):
            block = row_block(z, k, i)
            rows = slice(i * B, (i + 1) * B)

            @pl.when((block == 0) & ((z != 0) | (x >= 2)))
            def _():
                own[rows, :] = jnp.zeros((B, B), jnp.float32)
                oth[rows, :] = jnp.zeros((B, B), jnp.float32)

            @pl.when((block == 1) & (z != 0))
            def _():
                part = mul((xh[rows, : 4 * B], xl[rows, : 4 * B]), (ah[...], al[...]), True)
                own[rows, :] = part[:, :B]
                oth[rows, :] = part[:, B:]

    half = jax.ShapeDtypeStruct((8 * B, B), jnp.float32)
    return pl.pallas_call(
        body,
        out_shape=(half, half),
        in_specs=[SMEM] + [VMEM] * (len(arrays) + 4),
        out_specs=(VMEM, VMEM),
        scratch_shapes=[pltpu.VMEM((8 * B, 8 * B), jnp.bfloat16)] * 2,
        compiler_params=params(20),
        cost_estimate=cost(8, 7),
        name="product",
    )(pos, *arrays, *zs)


def finish(pos, a, own, got):
    def body(pos_ref, a_ref, own_ref, got_ref, out_ref):
        z, k = pos_ref[0], pos_ref[2]
        for i in range(8):
            for core, ref in ((k, own_ref), (1 - k, got_ref)):
                block = row_block(z, core, i)
                out_ref[block] = jnp.where(z == 0, 0.0, a_ref[block]) - ref[i]

    return pl.pallas_call(
        body,
        out_shape=jax.ShapeDtypeStruct((2 * Z, B, B), jnp.float32),
        in_specs=[SMEM] + [VMEM] * 3,
        out_specs=VMEM,
        compiler_params=params(8),
        cost_estimate=cost(0, 3),
        name="finish",
    )(pos, a, own.reshape(Z, B, B), got.reshape(Z, B, B))


def shards(matrix, inverse_factors):
    z, x, k, y = (lax.axis_index(n) for n in ("z", "x", "k", "y"))
    pos = jnp.stack([z, x, k, y]).astype(jnp.int32)
    a = matrix.reshape(16, B, B)

    def around(v, axis, size):
        perm = [(2 * i, 2 * ((i + 1) % size)) for i in range(size)]
        perm += [(2 * i + 1, 2 * ((i - 1) % size) + 1) for i in range(size)]
        return lax.ppermute(v, (axis, "k"), perm)

    blocks = jnp.swapaxes(a[:2], 1, 2)
    f0, g0 = swap(blocks, FIRST), swap(blocks, SECOND)

    theirs = other_core(blocks)
    columns = jnp.where(k == 0, jnp.concatenate([blocks, theirs]), jnp.concatenate([theirs, blocks]))
    corner = jnp.where(x < 2, columns[1::2], columns[::2])

    def to_core1(v, pairs):
        return lax.ppermute(v, ("z", "k"), [(2 * i + c, 2 * j + 1) for i, c, j in pairs])

    near, far = to_core1(corner, [(0, 0, 4), (0, 1, 2)]), to_core1(corner, [(0, 0, 6)])
    fg = jnp.stack([f0, g0])
    slab = jnp.stack([fg, other_core(fg)])
    r1 = around(slab, "z", Z)
    s0 = around(fg, "x", X)
    corner = jnp.where((z == 4) | (z == 2), near, jnp.where(z == 6, far, corner))
    corner = jnp.where(z % 2 == 1, to_core1(corner, [(0, 0, 1), (2, 1, 3), (4, 1, 5), (6, 1, 7)]), corner)
    beside = lax.ppermute(corner, ("x", "k"), [(2 * i + 1, 2 * (i ^ 1) + 1) for i in range(X)])
    gathered = gather_y(jnp.where(k == 0, columns, jnp.concatenate([corner, beside])))

    r2 = around(r1, "z", Z)
    s1 = around(r1, "x", X)
    r3 = around(r2, "z", Z)
    s2 = around(r2, "x", X)
    zs = factor(pos, inverse_factors, gathered, other_core(jnp.stack(gathered)))
    r4 = around(r3[0], "z", Z)
    s3 = around(r3, "x", X)
    s4 = around(after(r4, *zs), "x", X)

    def piece(ring, side, *at):
        return [((ring, side)[j // 2], *at, j % 2, p) for p in range(2) for j in range(4)]

    pieces = [piece(fg, s0)]
    for ring, side in ((r1, s1), (r2, s2), (r3, s3)):
        pieces += [piece(ring, side, 0), piece(ring, side, 1)]
    pieces += [piece(r4, s4)]

    own, other = product(pos, pieces, zs)
    return finish(pos, a, own, other_core(other)).reshape(16, B, 1, B)


def solution(mesh):
    fine = Mesh(mesh.devices.reshape(Z, X, K, Y), ("z", "x", "k", "y"))
    spec = P(None, "y", None, ("z", "x", "k"))
    return jax.shard_map(shards, mesh=fine, in_specs=(spec, P()), out_specs=spec, check_vma=False)
```
